128 devices in a mesh: row: 8 (over x, z_hi), col: 16 (over z_lo, y, core).
Axes of the slice: x: 4, y: 4, z: 4 (z_hi: 2, z_lo: 2; z = z_hi * 2 + z_lo), core: 2. Of those that a mesh axis runs over, the one named last changes fastest.
Arguments:
- coeffs: bfloat16 [128, 512, 128], P(('row', 'col')), may hold values from -6 to 6
- trial: bfloat16 [128, 32, 128], P(('row', 'col')), may hold values from -6 to 6
- screened: bfloat16 [128, 512, 512], P('col'), may hold values from -9.1552734e-05 to 9.1552734e-05
- qmap: int32 [128, 128], replicated, may hold values from 0 to 127, as said below
- mask: int32 [128, 128], replicated, may hold values from 0 to 1, as said below
Outputs:
- product: float32 [128, 32, 128], P(('row', 'col'))
The draws below stay inside these ranges and needn't reach their ends.
Inputs may be any that keep to these rules, and one draw needn't show every extreme that they name: qmap[k, k'] depends on k - k' modulo 128 only. Over the pairs (k, k') of one tile of 16 rows by 8 columns at offsets that are multiples of 16 and 8, at most 2 distinct values fall in any group q // 8; the same holds for the pairs (k', k); some tile reaches 2. mask[k, k] = 1 and mask[k, k'] + mask[k', k] = 1 for k != k'.
All inputs are finite; a program needn't handle non-finite values.
Results may differ from the reference program's by a relative error of at most 0.004.
Values may be sent and summed in bfloat16 or wider, within the bound.
A program may use at most 192 MiB of HBM per device.

```python
import jax
import jax.numpy as jnp
from jax import lax

NT = 128
R = 512
NV = 32
NK = 128
NQ = 128
QC = 8


def draw_qmap(key, part):
    offset = jax.random.randint(jax.random.fold_in(key, 11), (), 0, NQ)
    rows_k = jnp.arange(NK, dtype=jnp.int32)[:, None]
    cols_k = jnp.arange(NK, dtype=jnp.int32)[None, :]
    differ = (rows_k - cols_k + offset + NQ) % NQ
    groups = NQ // QC
    return (differ % groups * QC + differ // groups).astype(jnp.int32)


def draw_mask(key, part):
    coins = jax.random.randint(jax.random.fold_in(key, 23), (NK, NK), 0, 2).astype(jnp.int32)
    rows_k = jnp.arange(NK, dtype=jnp.int32)[:, None]
    cols_k = jnp.arange(NK, dtype=jnp.int32)[None, :]
    lower = 1 - jnp.transpose(coins)
    return jnp.where(rows_k < cols_k, coins, jnp.where(rows_k > cols_k, lower, 1)).astype(jnp.int32)


def block_scale(rng, shape, cuts, least, high):
    level, own = 1.0, jax.random.fold_in(rng, 6)
    for dim, blocks in cuts:
        draws = jnp.exp(jax.random.uniform(jax.random.fold_in(own, dim), (blocks,), jnp.float32, least / len(cuts), high / len(cuts)))
        level = level * jnp.repeat(draws, shape[dim] // blocks).reshape([-1 if axis == dim else 1 for axis in range(len(shape))])
    return level


def gaussian(own_key, extent, scale, reach, cuts=(), kind=jnp.bfloat16):
    values = jax.random.normal(own_key, extent, jnp.float32) * scale
    if len(cuts) > 0:
        values = block_scale(own_key, extent, cuts, -0.22, 0.18) * values
    return jnp.clip(values, min=-reach, max=reach).astype(kind)


def setup_inputs(seed: int = 0) -> dict:
    key_list = jax.random.split(jax.random.key(seed), 6)
    coeffs = gaussian(key_list[0], (NK, R, NT), 1.0, 6.0, ((0, 128),))
    trial = gaussian(key_list[1], (NK, NV, NT), 1.0, 6.0, ((0, 128),))
    screened = gaussian(key_list[2], (NQ, R, R), (R * R * NK * NT) ** -0.5, 9.1552734375e-05, ((0, 16),))
    qmap = draw_qmap(jax.random.fold_in(key_list[5], 71), 0)
    mask = draw_mask(jax.random.fold_in(key_list[5], 71), 0)
    return {"coeffs": coeffs, "trial": trial, "screened": screened, "qmap": qmap, "mask": mask}


def reference(coeffs, trial, screened, qmap, mask):
    total = coeffs.shape[0]
    columns = jnp.arange(total, dtype=jnp.int32)
    coeff_all = coeffs.astype(jnp.float32)
    trial_all = trial.astype(jnp.float32)

    def sweep(carry, index_row):
        coeff_row = coeff_all[index_row]
        picked = jnp.take(screened, qmap[index_row], axis=0).astype(jnp.float32)
        halves = jnp.einsum('rt,jrs->jts', coeff_row, picked).astype(jnp.bfloat16)
        blocks = jnp.einsum('jts,jsu->jtu', halves.astype(jnp.float32), coeff_all).astype(jnp.bfloat16)
        block_f = blocks.astype(jnp.float32)
        mask_row = mask[index_row].astype(jnp.float32)
        forward = jnp.einsum('j,jtu,jvu->vt', mask_row, block_f, trial_all)
        weight = jnp.where(columns != index_row, mask_row, jnp.float32(0.0))
        backward = jnp.einsum('j,jtu,vt->jvu', weight, block_f, trial_all[index_row])
        carry = carry + backward
        carry = carry.at[index_row].add(forward)
        return carry, None

    start = jnp.zeros(trial.shape, jnp.float32)
    result, _ = lax.scan(sweep, start, columns)
    return result
```

```python
import jax
import jax.numpy as jnp
from jax import lax
from jax.experimental import pallas as pl
from jax.experimental.pallas import tpu as pltpu
from jax.sharding import PartitionSpec as P


def apply_kernel(n_row_k, per_owner, qrow_hbm, mask_hbm, vecs_hbm, w_hbm, out_ref,
                 vecs, wbuf, qrow, masks, found, sems, wsems):
    total = vecs_hbm.shape[0]
    nv = vecs_hbm.shape[1]
    row_pos = lax.axis_index("row")
    col_pos = lax.axis_index("col")
    k0 = row_pos * n_row_k
    copies = [
        pltpu.make_async_copy(qrow_hbm.at[pl.ds(0, 1)], qrow, sems.at[0]),
        pltpu.make_async_copy(mask_hbm.at[pl.ds(k0, n_row_k)], masks, sems.at[1]),
        pltpu.make_async_copy(vecs_hbm, vecs.at[pl.ds(0, total)], sems.at[2]),
        pltpu.make_async_copy(vecs_hbm.at[pl.ds(0, n_row_k)], vecs.at[pl.ds(total, n_row_k)], sems.at[3]),
    ]
    for copy in copies:
        copy.start()
    wcopies = [pltpu.make_async_copy(w_hbm.at[j], wbuf.at[j], wsems.at[j]) for j in range(per_owner)]
    for copy in wcopies:
        copy.start()
    out_ref[...] = jnp.zeros_like(out_ref)
    copies[0].wait()
    copies[1].wait()

    def scan(d, count):
        q = qrow[0, lax.rem(total - d, total)]
        found[count] = d
        return count + (q // per_owner == col_pos).astype(jnp.int32)

    count = lax.fori_loop(0, total, scan, jnp.int32(0))
    copies[2].wait()
    copies[3].wait()
    for copy in wcopies:
        copy.wait()

    def side(start, weights):
        blocks = []
        for i in range(n_row_k):
            scale = jnp.full((nv, vecs.shape[2]), weights[i], jnp.float32).astype(jnp.bfloat16)
            blocks.append(vecs[start + i] * scale)
        return jnp.concatenate(blocks, axis=0)

    def step(j, carry):
        d = found[j]
        q = qrow[0, lax.rem(total - d, total)]
        w = wbuf[q - col_pos * per_owner]
        ahead, behind = [], []
        for i in range(n_row_k):
            ahead.append(masks[i, lax.rem(k0 + i + total - d, total)].astype(jnp.float32))
            mirror = 1 - masks[i, lax.rem(k0 + i + d, total)]
            behind.append(jnp.where(d == 0, 0, mirror).astype(jnp.float32))
        direct = side(lax.rem(k0 + total - d, total), ahead)
        out_ref[...] += lax.dot_general(
            direct, w, (((1,), (1,)), ((), ())), preferred_element_type=jnp.float32
        )
        turned = side(lax.rem(k0 + d, total), behind)
        out_ref[...] += jnp.dot(turned, w, preferred_element_type=jnp.float32)
        return carry

    lax.fori_loop(0, count, step, 0)


def apply(qmap, mask, vecs, screened, n_row_k):
    total, nv, rank = vecs.shape
    per_owner = screened.shape[0]
    return pl.pallas_call(
        lambda *refs: apply_kernel(n_row_k, per_owner, *refs),
        out_shape=jax.ShapeDtypeStruct((n_row_k * nv, rank), jnp.float32),
        in_specs=[pl.BlockSpec(memory_space=pl.ANY)] * 4,
        out_specs=pl.BlockSpec(memory_space=pltpu.VMEM),
        scratch_shapes=[
            pltpu.VMEM((total + n_row_k, nv, rank), jnp.bfloat16),
            pltpu.VMEM((per_owner, rank, rank), jnp.bfloat16),
            pltpu.SMEM((1, total), jnp.int32),
            pltpu.SMEM((n_row_k, total), jnp.int32),
            pltpu.SMEM((total + 1,), jnp.int32),
            pltpu.SemaphoreType.DMA((4,)),
            pltpu.SemaphoreType.DMA((per_owner,)),
        ],
        compiler_params=pltpu.CompilerParams(vmem_limit_bytes=40 * 2**20),
    )(qmap, mask, vecs, screened)


def per_device(coeffs, trial, screened, qmap, mask):
    n_col = lax.axis_size("col")
    vec = jnp.einsum("vu,ru->vr", trial[0], coeffs[0], preferred_element_type=jnp.float32)
    vecs = lax.all_gather(vec.astype(jnp.bfloat16), ("row", "col"))
    partial = apply(qmap, mask, vecs, screened, n_col)
    partial = partial.reshape(n_col, vec.shape[0], vec.shape[1])
    own = lax.psum_scatter(partial, "col", scatter_dimension=0)
    high = own.astype(jnp.bfloat16)
    low = (own - high.astype(jnp.float32)).astype(jnp.bfloat16)
    out = jnp.einsum("vr,rt->vt", high, coeffs[0], preferred_element_type=jnp.float32)
    out += jnp.einsum("vr,rt->vt", low, coeffs[0], preferred_element_type=jnp.float32)
    return out[None]


def solution(mesh):
    return jax.shard_map(
        per_device,
        mesh=mesh,
        in_specs=(
            P(("row", "col"), None, None),
            P(("row", "col"), None, None),
            P("col", None, None),
            P(),
            P(),
        ),
        out_specs=P(("row", "col"), None, None),
        check_vma=False,
    )
```

```python
import jax
import jax.numpy as jnp
from jax import lax
from jax.experimental import pallas as pl
from jax.experimental.pallas import tpu as pltpu
from jax.sharding import PartitionSpec as P


def apply_kernel(n_row_k, per_owner, qrow_hbm, mask_hbm, vecs, w_ref, out_ref,
                 qrow, masks, found, sems):
    total, nv, rank = vecs.shape
    row_pos = lax.axis_index("row")
    col_pos = lax.axis_index("col")
    k0 = row_pos * n_row_k
    copies = [
        pltpu.make_async_copy(qrow_hbm.at[pl.ds(0, 1)], qrow, sems.at[0]),
        pltpu.make_async_copy(mask_hbm.at[pl.ds(k0, n_row_k)], masks, sems.at[1]),
    ]
    for copy in copies:
        copy.start()
    out_ref[...] = jnp.zeros_like(out_ref)
    for copy in copies:
        copy.wait()

    def scan(d, count):
        q = qrow[0, lax.rem(total - d, total)]
        found[count] = d
        return count + (q // per_owner == col_pos).astype(jnp.int32)

    count = lax.fori_loop(0, total, scan, jnp.int32(0))

    def side(start, weights):
        blocks = []
        for i in range(n_row_k):
            scale = jnp.full((nv, rank), weights[i], jnp.float32).astype(jnp.bfloat16)
            blocks.append(vecs[lax.rem(start + i, total)] * scale)
        return jnp.concatenate(blocks, axis=0)

    def step(j, carry):
        d = found[j]
        q = qrow[0, lax.rem(total - d, total)]
        w = w_ref[q - col_pos * per_owner]
        ahead, behind = [], []
        for i in range(n_row_k):
            ahead.append(masks[i, lax.rem(k0 + i + total - d, total)].astype(jnp.float32))
            mirror = 1 - masks[i, lax.rem(k0 + i + d, total)]
            behind.append(jnp.where(d == 0, 0, mirror).astype(jnp.float32))
        direct = side(k0 + total - d, ahead)
        out_ref[...] += lax.dot_general(
            direct, w, (((1,), (1,)), ((), ())), preferred_element_type=jnp.float32
        )
        turned = side(k0 + d, behind)
        out_ref[...] += jnp.dot(turned, w, preferred_element_type=jnp.float32)
        return carry

    lax.fori_loop(0, count, step, 0)


def apply(qmap, mask, vecs, screened, n_row_k):
    total, nv, rank = vecs.shape
    per_owner = screened.shape[0]
    vmem = pl.BlockSpec(memory_space=pltpu.VMEM)
    return pl.pallas_call(
        lambda *refs: apply_kernel(n_row_k, per_owner, *refs),
        out_shape=jax.ShapeDtypeStruct((n_row_k * nv, rank), jnp.float32),
        in_specs=[pl.BlockSpec(memory_space=pl.ANY)] * 2 + [vmem] * 2,
        out_specs=vmem,
        scratch_shapes=[
            pltpu.SMEM((1, total), jnp.int32),
            pltpu.SMEM((n_row_k, total), jnp.int32),
            pltpu.SMEM((total + 1,), jnp.int32),
            pltpu.SemaphoreType.DMA((2,)),
        ],
        compiler_params=pltpu.CompilerParams(vmem_limit_bytes=24 * 2**20),
    )(qmap, mask, vecs, screened)


MESH = pl.DeviceIdType.MESH
SIDE = 4
PARTS = (
    ((0, 16), (0, 384), "yzx"),
    ((16, 16), (0, 384), "xzy"),
    ((0, 32), (384, 128), "xyz"),
)


def position():
    row, col = lax.axis_index("row"), lax.axis_index("col")
    return {"x": row // 2, "z": row % 2 * 2 + col // 8, "y": col % 8 // 2}, col % 2


def device(at, core):
    return (at["x"] * 2 + at["z"] // 2, at["z"] % 2 * 8 + at["y"] * 2 + core)


def moved(at, dim, by):
    return {**at, dim: lax.rem(at[dim] + SIDE + by, SIDE)}


def greet(peers):
    barrier = pltpu.get_barrier_semaphore()
    for peer in peers:
        pl.semaphore_signal(barrier, inc=1, device_id=peer, device_id_type=MESH)
    pl.semaphore_wait(barrier, len(peers))


def gather_kernel(coeffs, trial, buf, own, local_sem, send_sems, recv_sems):
    at, core = position()
    own[...] = lax.dot_general(
        trial[0], coeffs[0], (((1,), (1,)), ((), ())), preferred_element_type=jnp.float32
    ).astype(own.dtype)
    greet([device(moved(at, dim, by), core) for dim in "xyz" for by in (1, -1)] + [device(at, 1 - core)])
    started = []

    def push(src, dst, to):
        k = len(started)
        copy = pltpu.make_async_remote_copy(
            src, dst, send_sems.at[k], recv_sems.at[k], device_id=to, device_id_type=MESH
        )
        copy.start()
        started.append(copy)
        return copy

    def region(spans, part):
        rows, cols, _ = part
        return buf.at[
            pl.ds(*spans["x"]), pl.ds(*spans["z"]), pl.ds(*spans["y"]), core, pl.ds(*rows), pl.ds(*cols)
        ]

    here = buf.at[at["x"], at["z"], at["y"], core]
    keep = pltpu.make_async_copy(own, here, local_sem)
    keep.start()
    first = {}
    for part in PARTS:
        rows, cols, order = part
        piece = own.at[pl.ds(*rows), pl.ds(*cols)]
        target = here.at[pl.ds(*rows), pl.ds(*cols)]
        first[part] = tuple(push(piece, target, device(moved(at, order[0], by), core)) for by in (1, -1))
    shared = [push(own, here, device(at, 1 - core))]
    keep.wait()
    for stage in range(3):
        waiting = {}
        for part in PARTS:
            order = part[2]
            dim = order[stage]
            if stage == 0:
                waiting[part] = first[part]
                continue
            spans = {d: (0, SIDE) if d in order[:stage] else (at[d], 1) for d in "xyz"}
            block = region(spans, part)
            waiting[part] = tuple(push(block, block, device(moved(at, dim, by), core)) for by in (1, -1))
        relays = {}
        for part in PARTS:
            order = part[2]
            dim = order[stage]
            up, down = (device(moved(at, dim, by), core) for by in (1, -1))
            spans = {d: (0, SIDE) if d in order[:stage] else (at[d], 1) for d in "xyz"}
            before = {**spans, dim: (moved(at, dim, -1)[dim], 1)}
            after = {**spans, dim: (moved(at, dim, 1)[dim], 1)}
            half = [before, after]
            if stage > 0:
                half = [{**before, order[0]: (0, SIDE // 2)}, {**after, order[0]: (SIDE // 2, SIDE // 2)}]
            waiting[part][0].wait_recv()
            block = region(half[0], part)
            relays[part] = [push(block, block, up)]
            waiting[part][1].wait_recv()
            if stage > 0:
                block = region(half[1], part)
                relays[part].append(push(block, block, down))
            for spans in (before, after):
                block = region(spans, part)
                shared.append(push(block, block, device(at, 1 - core)))
        for part in PARTS:
            order = part[2]
            dim = order[stage]
            spans = {d: (0, SIDE) if d in order[:stage] else (at[d], 1) for d in "xyz"}
            for copy in relays[part]:
                copy.wait_recv()
            block = region({**spans, dim: (moved(at, dim, 2)[dim], 1)}, part)
            shared.append(push(block, block, device(at, 1 - core)))
    for copy in shared:
        copy.wait_recv()
    for copy in started:
        copy.wait_send()


def gather(coeffs, trial):
    nv, rank = trial.shape[1], coeffs.shape[1]
    copies = 61
    vmem = pl.BlockSpec(memory_space=pltpu.VMEM)
    return pl.pallas_call(
        gather_kernel,
        out_shape=jax.ShapeDtypeStruct((SIDE, SIDE, SIDE, 2, nv, rank), jnp.bfloat16),
        in_specs=[vmem, vmem],
        out_specs=pl.BlockSpec(memory_space=pl.ANY),
        scratch_shapes=[
            pltpu.VMEM((nv, rank), jnp.bfloat16),
            pltpu.SemaphoreType.DMA,
            pltpu.SemaphoreType.DMA((copies,)),
            pltpu.SemaphoreType.DMA((copies,)),
        ],
        compiler_params=pltpu.CompilerParams(
            collective_id=0, has_side_effects=True, vmem_limit_bytes=4 * 2**20
        ),
    )(coeffs, trial)


def reduce_kernel(partial, coeffs, out, pair, staged, landed, pair_send, pair_recv, send_sems, recv_sems):
    at, core = position()
    zl, y = at["z"] % 2, at["y"]
    row = lax.axis_index("row")
    steps = [(a, b) for b in (2, 1, 3, 0) for a in (1, 0)]

    def there(a, b):
        return lax.rem(zl + a, 2), lax.rem(y + b, SIDE)

    def peer(a, b, c):
        far_z, far_y = there(a, b)
        return (row, far_z * 8 + far_y * 2 + c)

    greet([peer(a, b, core) for a, b in steps if (a, b) != (0, 0)] + [peer(0, 0, 1 - core)])
    swaps = []
    for k, (a, b) in enumerate(steps):
        far_z, far_y = there(a, b)
        swap = pltpu.make_async_remote_copy(
            partial.at[far_z, far_y, 1 - core], pair.at[k], pair_send.at[k], pair_recv.at[k],
            device_id=peer(0, 0, 1 - core), device_id_type=MESH,
        )
        swap.start()
        swaps.append(swap)
    sends = []

    def post(k):
        send = pltpu.make_async_remote_copy(
            staged.at[k], landed.at[k], send_sems.at[k], recv_sems.at[k],
            device_id=peer(*steps[k], core), device_id_type=MESH,
        )
        send.start()
        sends.append(send)

    total = None
    for k, (a, b) in enumerate(steps):
        far_z, far_y = there(a, b)
        swaps[k].wait_recv()
        both = partial[far_z, far_y, core] + pair[k]
        if (a, b) == (0, 0):
            total = both
        else:
            staged[k] = both.astype(staged.dtype)
        if k > 0:
            post(k - 1)
    for k, send in enumerate(sends):
        send.wait_recv()
        total += landed[k].astype(jnp.float32)
    high = total.astype(jnp.bfloat16)
    low = (total - high.astype(jnp.float32)).astype(jnp.bfloat16)
    out[0] = jnp.dot(high, coeffs[0], preferred_element_type=jnp.float32) + jnp.dot(
        low, coeffs[0], preferred_element_type=jnp.float32
    )
    for copy in swaps + sends:
        copy.wait_send()


def reduce(partial, coeffs):
    nv, rank, nt = partial.shape[-2], partial.shape[-1], coeffs.shape[2]
    vmem = pl.BlockSpec(memory_space=pltpu.VMEM)
    return pl.pallas_call(
        reduce_kernel,
        out_shape=jax.ShapeDtypeStruct((1, nv, nt), jnp.float32),
        in_specs=[vmem, vmem],
        out_specs=vmem,
        scratch_shapes=[
            pltpu.VMEM((8, nv, rank), jnp.float32),
            pltpu.VMEM((7, nv, rank), jnp.bfloat16),
            pltpu.VMEM((7, nv, rank), jnp.bfloat16),
            pltpu.SemaphoreType.DMA((8,)),
            pltpu.SemaphoreType.DMA((8,)),
            pltpu.SemaphoreType.DMA((7,)),
            pltpu.SemaphoreType.DMA((7,)),
        ],
        compiler_params=pltpu.CompilerParams(
            collective_id=1, has_side_effects=True, vmem_limit_bytes=8 * 2**20
        ),
    )(partial, coeffs)


def per_device(coeffs, trial, screened, qmap, mask):
    n_col = lax.axis_size("col")
    nv, rank = trial.shape[1], coeffs.shape[1]
    vecs = gather(coeffs, trial).reshape(-1, nv, rank)
    partial = apply(qmap, mask, vecs, screened, n_col)
    return reduce(partial.reshape(2, SIDE, 2, nv, rank), coeffs)


def solution(mesh):
    return jax.shard_map(
        per_device,
        mesh=mesh,
        in_specs=(
            P(("row", "col"), None, None),
            P(("row", "col"), None, None),
            P("col", None, None),
            P(),
            P(),
        ),
        out_specs=P(("row", "col"), None, None),
        check_vma=False,
    )
```

```python
import jax
import jax.numpy as jnp
from jax import lax
from jax.experimental import pallas as pl
from jax.experimental.pallas import tpu as pltpu
from jax.sharding import PartitionSpec as P


MESH = pl.DeviceIdType.MESH
SIDE = 4
PARTS = (
    ((0, 16), (0, 384), "yzx"),
    ((16, 16), (0, 384), "zxy"),
    ((0, 32), (384, 128), "xyz"),
)
NEAR = (0, 1, -1, 2)
UP, DOWN = (0, 2), (1, -1)


def position():
    row, col = lax.axis_index("row"), lax.axis_index("col")
    return {"x": row // 2, "z": row % 2 * 2 + col // 8, "y": col % 8 // 2}, col % 2


def device(at, core):
    return (at["x"] * 2 + at["z"] // 2, at["z"] % 2 * 8 + at["y"] * 2 + core)


def moved(at, dim, by):
    return {**at, dim: lax.rem(at[dim] + SIDE + by, SIDE)}


def greet(peers):
    barrier = pltpu.get_barrier_semaphore()
    for peer in peers:
        pl.semaphore_signal(barrier, inc=1, device_id=peer, device_id_type=MESH)
    return lambda: pl.semaphore_wait(barrier, len(peers))


def one_round(n_slots, n_row_k, turn, coeffs_hbm, trial_hbm, w_hbm, q_hbm, mask_hbm, out, most,
              coeffs, trial, own, part0, part1, part2, vecs, weights, acc, pair, staged, landed,
              qrow, qvec, masks, slots, load_sems, local_sems, send_sems, recv_sems):
    at, core = position()
    partner = device(at, 1 - core)
    row, col = lax.axis_index("row"), lax.axis_index("col")
    zl, y = at["z"] % 2, at["y"]
    spread = [(a, b) for b in (2, 1, 3, 0) for a in (1, 0)]

    def there(a, b):
        return lax.rem(zl + a, 2), lax.rem(y + b, SIDE)

    def peer(a, b):
        far_z, far_y = there(a, b)
        return (row, far_z * 8 + far_y * 2 + core)

    meet = greet(
        [device(moved(at, dim, by), core) for dim in "xyz" for by in (1, -1, 2)]
        + [partner] + [peer(1, b) for b in (1, 2, 3)]
    )
    k0 = row * n_row_k
    total = q_hbm.shape[1]
    rows = mask_hbm.at[pl.ds(k0, n_row_k)]
    loads = [
        pltpu.make_async_copy(coeffs_hbm, coeffs, load_sems.at[0]),
        pltpu.make_async_copy(trial_hbm, trial, load_sems.at[1]),
        pltpu.make_async_copy(q_hbm.at[pl.ds(0, 1)], qrow, load_sems.at[2]),
        pltpu.make_async_copy(rows, masks.at[:, pl.ds(0, total)], load_sems.at[3]),
        pltpu.make_async_copy(rows, masks.at[:, pl.ds(total, total)], load_sems.at[4]),
        pltpu.make_async_copy(w_hbm, weights, load_sems.at[5]),
        pltpu.make_async_copy(q_hbm.at[pl.ds(0, 1)], qvec, load_sems.at[6]),
    ]
    for load in loads:
        load.start()
    for load in loads[:2]:
        load.wait()
    own[...] = lax.dot_general(
        trial[0], coeffs[0], (((1,), (1,)), ((), ())), preferred_element_type=jnp.float32
    ).astype(own.dtype)
    bufs = (part0, part1, part2)
    started, shared, local = [], [], []
    arrivals = {}

    def push(src, dst, to):
        k = len(started)
        copy = pltpu.make_async_remote_copy(
            src, dst, send_sems.at[k], recv_sems.at[k], device_id=to, device_id_type=MESH
        )
        copy.start()
        started.append(copy)
        return copy

    def keep(src, dst):
        copy = pltpu.make_async_copy(src, dst, local_sems.at[len(local)])
        copy.start()
        local.append(copy)

    def coords(n, steps):
        order = PARTS[n][2]
        return {d: None if by is None else moved(at, d, by)[d] for d, by in zip(order, steps)}

    def region(n, steps):
        place = coords(n, steps)
        return bufs[n].at[tuple(place[d] for d in PARTS[n][2][::-1] if place[d] is not None)]

    def final(n, steps):
        place = coords(n, steps)
        rows, cols = PARTS[n][:2]
        spans = tuple(pl.ds(0, SIDE) if place[d] is None else place[d] for d in "xzy")
        return vecs.at[spans + (core, pl.ds(*rows), pl.ds(*cols))]

    def place(n, steps):
        src, dst = region(n, steps), final(n, steps)
        shared.append(push(src, dst, partner))
        keep(src, dst)

    def send(n, stage, by, steps, src=None):
        dim = PARTS[n][2][stage]
        block = region(n, steps)
        copy = push(block if src is None else src, block, device(moved(at, dim, by), core))
        came = list(steps)
        came[stage] = (steps[stage] - by + 1) % SIDE - 1
        arrivals[n, tuple(came)] = copy

    def arrived(n, steps):
        arrivals[n, steps].wait_recv()

    def prepare():
        for load in loads[2:5]:
            load.wait()
        base = col * n_slots
        skip = turn[0] * n_slots

        def scan(j, carry):
            count, picked = carry
            q = qrow[0, j]
            held = (q >= base) & (q < base + n_slots)
            picked = tuple(jnp.where(held & (count == n), j, p) for n, p in enumerate(picked))
            return count + jnp.where(held, 1, 0), picked

        first = (-skip, (jnp.int32(-1),) * n_slots)
        _, picked = lax.fori_loop(0, total, scan, first, unroll=4)
        for n, p in enumerate(picked):
            slots[n] = p
        acc[...] = jnp.zeros_like(acc)
        loads[6].wait()
        first_q = n_slots * lax.broadcasted_iota(jnp.int32, (n_row_k, total), 0)
        held = (qvec[...] >= first_q) & (qvec[...] < first_q + n_slots)
        counts = jnp.sum(jnp.where(held, 1.0, 0.0), axis=1, keepdims=True)
        most[0] = jnp.max(counts).astype(jnp.int32)

    parts = range(len(PARTS))
    own_piece = [own.at[pl.ds(*PARTS[n][0]), pl.ds(*PARTS[n][1])] for n in parts]
    for n in parts:
        keep(own_piece[n], region(n, (0, 0, 0)))
    meet()
    for by in (2, 1, -1):
        for n in parts:
            send(n, 0, by, (0, 0, 0), own_piece[n])
    for by in (2, 1, -1):
        for n in parts:
            send(n, 1, by, (0, 0, 0), own_piece[n])
    for copy in local:
        copy.wait()
    del local[:]
    for near in (1, -1, 2):
        for n in parts:
            arrived(n, (near, 0, 0))
            for by in (2, 1, -1):
                send(n, 1, by, (near, 0, 0))
    for near in NEAR:
        for n in parts:
            if near != 0:
                for first in NEAR:
                    arrived(n, (first, near, 0))
            for by in (1, -1):
                send(n, 2, by, (None, near, 0))
            place(n, (None, near, 0))
    prepare()
    for near in NEAR:
        for n in parts:
            for by in (1, -1):
                arrived(n, (None, near, -by))
                if near in (UP if by == 1 else DOWN):
                    send(n, 2, by, (None, near, -by))
                place(n, (None, near, -by))
    for near in NEAR:
        for n in parts:
            arrived(n, (None, near, 2))
            place(n, (None, near, 2))
    for copy in shared:
        copy.wait_recv()
    for copy in local:
        copy.wait()
    loads[5].wait()
    nv, rank = own.shape

    def wrapped(k):
        return jnp.where(k >= total, k - total, k)

    def side(start, scales):
        blocks = []
        for i in range(n_row_k):
            scale = jnp.full((nv, rank), scales[i], jnp.float32).astype(own.dtype)
            blocks.append(flat[wrapped(start + i)] * scale)
        return jnp.concatenate(blocks, axis=0)

    flat = vecs.reshape(total, nv, rank)

    def step(n, carry):
        slot = slots[n]
        used = jnp.where(slot >= 0, 1, 0)
        j = jnp.where(slot >= 0, slot, 0)
        w = weights[jnp.where(slot >= 0, qrow[0, j] - col * n_slots, 0)]
        ahead_k = wrapped(k0 + j)
        behind_k = wrapped(k0 + total - j)
        turned_used = jnp.where(slot > 0, 1, 0)
        ahead = [(used * masks[i, ahead_k + i]).astype(jnp.float32) for i in range(n_row_k)]
        behind = [(turned_used * (1 - masks[i, behind_k + i])).astype(jnp.float32) for i in range(n_row_k)]
        direct = side(ahead_k, ahead)
        turned = side(behind_k, behind)
        both = lax.dot_general(
            direct, w, (((1,), (1,)), ((), ())), preferred_element_type=jnp.float32
        ) + jnp.dot(turned, w, preferred_element_type=jnp.float32)
        acc[...] += both.reshape(acc.shape)
        return carry

    lax.fori_loop(0, n_slots, step, 0)

    def mate(k, c):
        far_z, far_y = there(*spread[k])
        return far_z * 8 + far_y * 2 + c

    swaps = [push(acc.at[mate(k, 1 - core)], pair.at[k], partner) for k in range(8)]
    sends = []

    def post(k):
        sends.append(push(staged.at[k], landed.at[k], peer(*spread[k])))

    for k in range(8):
        swaps[k].wait_recv()
        summed = acc[mate(k, core)] + pair[k]
        if k < 7:
            staged[k] = summed.astype(staged.dtype)
        if k > 0:
            post(k - 1)
    for k in range(7):
        sends[k].wait_recv()
        summed += landed[k].astype(jnp.float32)
    high = summed.astype(jnp.bfloat16)
    low = (summed - high.astype(jnp.float32)).astype(jnp.bfloat16)
    out[0] = jnp.dot(high, coeffs[0], preferred_element_type=jnp.float32) + jnp.dot(
        low, coeffs[0], preferred_element_type=jnp.float32
    )
    for copy in started:
        copy.wait_send()


def run_round(turn, coeffs, trial, screened, qmap, mask):
    nv, rank, nt = trial.shape[1], coeffs.shape[1], coeffs.shape[2]
    n_slots = screened.shape[0]
    n_row_k = lax.axis_size("col")
    total = qmap.shape[0]
    pieces, shares = 27 * len(PARTS), 16 * len(PARTS)
    remote = pieces + shares + 15
    anywhere = pl.BlockSpec(memory_space=pl.ANY)
    return pl.pallas_call(
        lambda *refs: one_round(n_slots, n_row_k, *refs),
        out_shape=(
            jax.ShapeDtypeStruct((1, nv, nt), jnp.float32),
            jax.ShapeDtypeStruct((1,), jnp.int32),
        ),
        in_specs=[pl.BlockSpec(memory_space=pltpu.SMEM)] + [anywhere] * 5,
        out_specs=(pl.BlockSpec(memory_space=pltpu.VMEM), pl.BlockSpec(memory_space=pltpu.SMEM)),
        scratch_shapes=[
            pltpu.VMEM(coeffs.shape, coeffs.dtype),
            pltpu.VMEM(trial.shape, trial.dtype),
            pltpu.VMEM((nv, rank), jnp.bfloat16),
        ]
        + [pltpu.VMEM((SIDE, SIDE, SIDE, part[0][1], part[1][1]), jnp.bfloat16) for part in PARTS]
        + [
            pltpu.VMEM((SIDE, SIDE, SIDE, 2, nv, rank), jnp.bfloat16),
            pltpu.VMEM(screened.shape, screened.dtype),
            pltpu.VMEM((n_row_k, nv, rank), jnp.float32),
            pltpu.VMEM((8, nv, rank), jnp.float32),
            pltpu.VMEM((7, nv, rank), jnp.bfloat16),
            pltpu.VMEM((7, nv, rank), jnp.bfloat16),
            pltpu.SMEM((1, total), jnp.int32),
            pltpu.VMEM((1, total), jnp.int32),
            pltpu.SMEM((n_row_k, 2 * total), jnp.int32),
            pltpu.SMEM((n_slots,), jnp.int32),
            pltpu.SemaphoreType.DMA((7,)),
            pltpu.SemaphoreType.DMA((shares,)),
            pltpu.SemaphoreType.DMA((remote,)),
            pltpu.SemaphoreType.DMA((remote,)),
        ],
        compiler_params=pltpu.CompilerParams(
            collective_id=0, has_side_effects=True, vmem_limit_bytes=60 * 2**20
        ),
    )(turn, coeffs, trial, screened, qmap, mask)


def per_device(coeffs, trial, screened, qmap, mask):
    n_slots = screened.shape[0]
    args = (coeffs, trial, screened, qmap, mask)
    first, most = run_round(jnp.zeros((1,), jnp.int32), *args)

    def more(state):
        return state[0] * n_slots < most[0]

    def again(state):
        return state[0] + 1, state[1] + run_round(state[0][None], *args)[0]

    return lax.while_loop(more, again, (jnp.int32(1), first))[1]


def solution(mesh):
    return jax.shard_map(
        per_device,
        mesh=mesh,
        in_specs=(
            P(("row", "col"), None, None),
            P(("row", "col"), None, None),
            P("col", None, None),
            P(),
            P(),
        ),
        out_specs=P(("row", "col"), None, None),
        check_vma=False,
    )
```

```python
import jax
import jax.numpy as jnp
from jax import lax
from jax.experimental import pallas as pl
from jax.experimental.pallas import tpu as pltpu
from jax.sharding import PartitionSpec as P


MESH = pl.DeviceIdType.MESH
SIDE = 4
HALVES = 2
PARTS = tuple(
    (h, (16 * h + r, n), cols, order, dims)
    for h in range(HALVES)
    for r, n, cols, order, dims in (
        (0, 8, (0, 384), "yzx", "xzy"),
        (8, 8, (0, 384), "zxy", "yxz"),
        (0, 16, (384, 128), "xyz", "zxy"),
    )
)


def position():
    row, col = lax.axis_index("row"), lax.axis_index("col")
    return {"x": row // 2, "z": row % 2 * 2 + col // 8, "y": col % 8 // 2}, col % 2


def device(at, core):
    return (at["x"] * 2 + at["z"] // 2, at["z"] % 2 * 8 + at["y"] * 2 + core)


def moved(at, dim, by):
    return {**at, dim: lax.rem(at[dim] + SIDE + by, SIDE)}


def greet(peers):
    barrier = pltpu.get_barrier_semaphore()
    for peer in peers:
        pl.semaphore_signal(barrier, inc=1, device_id=peer, device_id_type=MESH)
    return lambda: pl.semaphore_wait(barrier, len(peers))


def one_round(n_slots, n_row_k, turn, coeffs_hbm, trial_hbm, w_hbm, q_hbm, mask_hbm, out, most,
              coeffs, trial, own, *rest):
    bufs, rest = rest[: len(PARTS)], rest[len(PARTS) :]
    vecs, rest = rest[:HALVES], rest[HALVES:]
    (weights, acc, pair, staged, landed, qrow, qvec, masks, slots,
     load_sems, local_sems, send_sems, recv_sems) = rest
    at, core = position()
    partner = device(at, 1 - core)
    row, col = lax.axis_index("row"), lax.axis_index("col")
    zl, y = at["z"] % 2, at["y"]
    spread = [(a, b) for b in (2, 1, 3, 0) for a in (1, 0)]

    def there(a, b):
        return lax.rem(zl + a, 2), lax.rem(y + b, SIDE)

    def peer(a, b):
        far_z, far_y = there(a, b)
        return (row, far_z * 8 + far_y * 2 + core)

    meet = greet(
        [device(moved(at, dim, by), core) for dim in "xyz" for by in (1, -1, 2)]
        + [partner] + [peer(1, b) for b in (1, 2, 3)]
    )
    k0 = row * n_row_k
    total = q_hbm.shape[1]
    rows = mask_hbm.at[pl.ds(k0, n_row_k)]
    loads = [
        pltpu.make_async_copy(coeffs_hbm, coeffs, load_sems.at[0]),
        pltpu.make_async_copy(trial_hbm, trial, load_sems.at[1]),
        pltpu.make_async_copy(q_hbm.at[pl.ds(0, 1)], qrow, load_sems.at[2]),
        pltpu.make_async_copy(rows, masks.at[:, pl.ds(0, total)], load_sems.at[3]),
        pltpu.make_async_copy(rows, masks.at[:, pl.ds(total, total)], load_sems.at[4]),
        pltpu.make_async_copy(w_hbm, weights, load_sems.at[5]),
        pltpu.make_async_copy(q_hbm.at[pl.ds(0, 1)], qvec, load_sems.at[6]),
    ]
    for load in loads:
        load.start()
    for load in loads[:2]:
        load.wait()
    own[...] = lax.dot_general(
        trial[0], coeffs[0], (((1,), (1,)), ((), ())), preferred_element_type=jnp.float32
    ).astype(own.dtype)
    started, local = [], []

    def push(src, dst, to):
        k = len(started)
        copy = pltpu.make_async_remote_copy(
            src, dst, send_sems.at[k], recv_sems.at[k], device_id=to, device_id_type=MESH
        )
        copy.start()
        started.append(copy)
        return copy

    def keep(src, dst):
        copy = pltpu.make_async_copy(src, dst, local_sems.at[len(local)])
        copy.start()
        local.append(copy)
        return copy

    def coords(n, steps):
        return {d: None if by is None else moved(at, d, by)[d] for d, by in zip(PARTS[n][3], steps)}

    def region(n, steps):
        where = coords(n, steps)
        return bufs[n].at[tuple(pl.ds(0, SIDE) if where[d] is None else where[d] for d in PARTS[n][4])]

    def place(n, steps):
        where = coords(n, steps)
        h, rows, cols, _, _ = PARTS[n]
        spans = tuple(pl.ds(0, SIDE) if where[d] is None else where[d] for d in "xzy")
        dst = vecs[h].at[spans + (core, pl.ds(rows[0] - 16 * h, rows[1]), pl.ds(*cols))]
        src = region(n, steps)
        return push(src, dst, partner), keep(src, dst)

    def send(n, stage, steps, src=None):
        dim = PARTS[n][3][stage]
        block = region(n, steps)
        return [
            push(block if src is None else src, block, device(moved(at, dim, by), core)) for by in (2, 1, -1)
        ]

    def prepare():
        for load in loads[2:5]:
            load.wait()
        base = col * n_slots
        skip = turn[0] * n_slots

        def scan(j, carry):
            count, picked = carry
            q = qrow[0, j]
            held = (q >= base) & (q < base + n_slots)
            picked = tuple(jnp.where(held & (count == n), j, p) for n, p in enumerate(picked))
            return count + jnp.where(held, 1, 0), picked

        first = (-skip, (jnp.int32(-1),) * n_slots)
        _, picked = lax.fori_loop(0, total, scan, first, unroll=4)
        for n, p in enumerate(picked):
            slots[n] = p
        acc[...] = jnp.zeros_like(acc)
        loads[6].wait()
        first_q = n_slots * lax.broadcasted_iota(jnp.int32, (n_row_k, total), 0)
        held = (qvec[...] >= first_q) & (qvec[...] < first_q + n_slots)
        counts = jnp.sum(jnp.where(held, 1.0, 0.0), axis=1, keepdims=True)
        most[0] = jnp.max(counts).astype(jnp.int32)

    parts = range(len(PARTS))
    mine = [[n for n in parts if PARTS[n][0] == h] for h in range(HALVES)]
    own_piece = [own.at[pl.ds(*PARTS[n][1]), pl.ds(*PARTS[n][2])] for n in parts]
    kept = [keep(own_piece[n], region(n, (0, 0, 0))) for n in parts]
    meet()
    moving = [send(n, 0, (0, 0, 0), own_piece[n]) for n in parts]
    for copy in kept:
        copy.wait()
    for stage, steps in ((1, (None, 0, 0)), (2, (None, None, 0))):
        for n in parts:
            for copy in moving[n]:
                copy.wait_recv()
            moving[n] = send(n, stage, steps)
    placing = [[place(n, (None, None, 0)) for n in mine[h]] for h in range(HALVES)]
    prepare()

    def arrive(h):
        for n in mine[h]:
            for copy, by in zip(moving[n], (2, -1, 1)):
                copy.wait_recv()
                placing[h].append(place(n, (None, None, by)))

    def settle(h):
        for there_copy, here_copy in placing[h]:
            there_copy.wait_recv()
            here_copy.wait()

    nv, rank = own.shape
    part_v = nv // HALVES

    def wrapped(k):
        return jnp.where(k >= total, k - total, k)

    def step(h):
        flat = vecs[h].reshape(total, part_v, rank)

        def side(start, scales):
            blocks = []
            for i in range(n_row_k):
                scale = jnp.full((part_v, rank), scales[i], jnp.float32).astype(own.dtype)
                blocks.append(flat[wrapped(start + i)] * scale)
            return jnp.concatenate(blocks, axis=0)

        def body(n, carry):
            slot = slots[n]
            used = jnp.where(slot >= 0, 1, 0)
            j = jnp.where(slot >= 0, slot, 0)
            w = weights[jnp.where(slot >= 0, qrow[0, j] - col * n_slots, 0)]
            ahead_k = wrapped(k0 + j)
            behind_k = wrapped(k0 + total - j)
            turned_used = jnp.where(slot > 0, 1, 0)
            ahead = [(used * masks[i, ahead_k + i]).astype(jnp.float32) for i in range(n_row_k)]
            behind = [
                (turned_used * (1 - masks[i, behind_k + i])).astype(jnp.float32) for i in range(n_row_k)
            ]
            direct = side(ahead_k, ahead)
            turned = side(behind_k, behind)
            both = lax.dot_general(
                direct, w, (((1,), (1,)), ((), ())), preferred_element_type=jnp.float32
            ) + jnp.dot(turned, w, preferred_element_type=jnp.float32)
            acc[h] += both.reshape(acc.shape[1:])
            return carry

        return body

    def mate(k, c):
        far_z, far_y = there(*spread[k])
        return far_z * 8 + far_y * 2 + c

    def swap(h):
        return [push(acc.at[h, mate(k, 1 - core)], pair.at[h, k], partner) for k in range(8)]

    sends = []

    def collect(h, swaps):
        for k in range(8):
            swaps[k].wait_recv()
            summed = acc[h, mate(k, core)] + pair[h, k]
            if k < 7:
                staged[h, k] = summed.astype(staged.dtype)
            if k > 0:
                sends.append(push(staged.at[h, k - 1], landed.at[h, k - 1], peer(*spread[k - 1])))
        return summed

    def finish(h, summed):
        for k in range(7):
            sends[h * 7 + k].wait_recv()
            summed += landed[h, k].astype(jnp.float32)
        high = summed.astype(jnp.bfloat16)
        low = (summed - high.astype(jnp.float32)).astype(jnp.bfloat16)
        out[0, pl.ds(h * part_v, part_v), :] = jnp.dot(
            high, coeffs[0], preferred_element_type=jnp.float32
        ) + jnp.dot(low, coeffs[0], preferred_element_type=jnp.float32)

    first, second = n_slots * 2 // 8, n_slots * 4 // 8
    arrive(0)
    loads[5].wait()
    settle(0)
    lax.fori_loop(0, first, step(0), 0)
    arrive(1)
    lax.fori_loop(first, n_slots, step(0), 0)
    early = swap(0)
    settle(1)
    lax.fori_loop(0, second, step(1), 0)
    summed0 = collect(0, early)
    lax.fori_loop(second, n_slots, step(1), 0)
    summed1 = collect(1, swap(1))
    finish(0, summed0)
    finish(1, summed1)
    for copy in started:
        copy.wait_send()


def run_round(turn, coeffs, trial, screened, qmap, mask):
    nv, rank, nt = trial.shape[1], coeffs.shape[1], coeffs.shape[2]
    n_slots = screened.shape[0]
    n_row_k = lax.axis_size("col")
    total = qmap.shape[0]
    part_v = nv // HALVES
    local = 5 * len(PARTS)
    remote = 13 * len(PARTS) + 15 * HALVES
    anywhere = pl.BlockSpec(memory_space=pl.ANY)
    return pl.pallas_call(
        lambda *refs: one_round(n_slots, n_row_k, *refs),
        out_shape=(
            jax.ShapeDtypeStruct((1, nv, nt), jnp.float32),
            jax.ShapeDtypeStruct((1,), jnp.int32),
        ),
        in_specs=[pl.BlockSpec(memory_space=pltpu.SMEM)] + [anywhere] * 5,
        out_specs=(pl.BlockSpec(memory_space=pltpu.VMEM), pl.BlockSpec(memory_space=pltpu.SMEM)),
        scratch_shapes=[
            pltpu.VMEM(coeffs.shape, coeffs.dtype),
            pltpu.VMEM(trial.shape, trial.dtype),
            pltpu.VMEM((nv, rank), jnp.bfloat16),
        ]
        + [pltpu.VMEM((SIDE, SIDE, SIDE, part[1][1], part[2][1]), jnp.bfloat16) for part in PARTS]
        + [
            pltpu.VMEM((SIDE, SIDE, SIDE, 2, part_v, rank), jnp.bfloat16) for _ in range(HALVES)
        ]
        + [
            pltpu.VMEM(screened.shape, screened.dtype),
            pltpu.VMEM((HALVES, n_row_k, part_v, rank), jnp.float32),
            pltpu.VMEM((HALVES, 8, part_v, rank), jnp.float32),
            pltpu.VMEM((HALVES, 7, part_v, rank), jnp.bfloat16),
            pltpu.VMEM((HALVES, 7, part_v, rank), jnp.bfloat16),
            pltpu.SMEM((1, total), jnp.int32),
            pltpu.VMEM((1, total), jnp.int32),
            pltpu.SMEM((n_row_k, 2 * total), jnp.int32),
            pltpu.SMEM((n_slots,), jnp.int32),
            pltpu.SemaphoreType.DMA((7,)),
            pltpu.SemaphoreType.DMA((local,)),
            pltpu.SemaphoreType.DMA((remote,)),
            pltpu.SemaphoreType.DMA((remote,)),
        ],
        compiler_params=pltpu.CompilerParams(
            collective_id=0, has_side_effects=True, vmem_limit_bytes=60 * 2**20
        ),
    )(turn, coeffs, trial, screened, qmap, mask)


def per_device(coeffs, trial, screened, qmap, mask):
    n_slots = screened.shape[0]
    args = (coeffs, trial, screened, qmap, mask)
    first, most = run_round(jnp.zeros((1,), jnp.int32), *args)

    def more(state):
        return state[0] * n_slots < most[0]

    def again(state):
        return state[0] + 1, state[1] + run_round(state[0][None], *args)[0]

    return lax.while_loop(more, again, (jnp.int32(1), first))[1]


def solution(mesh):
    return jax.shard_map(
        per_device,
        mesh=mesh,
        in_specs=(
            P(("row", "col"), None, None),
            P(("row", "col"), None, None),
            P("col", None, None),
            P(),
            P(),
        ),
        out_specs=P(("row", "col"), None, None),
        check_vma=False,
    )
```

```python
import jax
import jax.numpy as jnp
from jax import lax
from jax.experimental import pallas as pl
from jax.experimental.pallas import tpu as pltpu
from jax.sharding import PartitionSpec as P


MESH = pl.DeviceIdType.MESH
SIDE = 4
HALVES = 2
PARTS = tuple(
    (h, (16 * h + r, n), cols, order, dims)
    for h in range(HALVES)
    for r, n, cols, order, dims in (
        (0, 8, (0, 384), "yzx", "xzy"),
        (8, 8, (0, 384), "zxy", "yxz"),
        (0, 16, (384, 128), "xyz", "zxy"),
    )
)


def position():
    row, col = lax.axis_index("row"), lax.axis_index("col")
    return {"x": row // 2, "z": row % 2 * 2 + col // 8, "y": col % 8 // 2}, col % 2


def device(at, core):
    return (at["x"] * 2 + at["z"] // 2, at["z"] % 2 * 8 + at["y"] * 2 + core)


def moved(at, dim, by):
    return {**at, dim: lax.rem(at[dim] + SIDE + by, SIDE)}


def greet(peers):
    barrier = pltpu.get_barrier_semaphore()
    for peer in peers:
        pl.semaphore_signal(barrier, inc=1, device_id=peer, device_id_type=MESH)
    return lambda: pl.semaphore_wait(barrier, len(peers))


def one_round(n_slots, n_row_k, turn, coeffs_hbm, trial_hbm, w_hbm, q_hbm, mask_hbm, out, most,
              coeffs, trial, own, *rest):
    bufs, rest = rest[: len(PARTS)], rest[len(PARTS) :]
    vecs, rest = rest[:HALVES], rest[HALVES:]
    (weights, acc, pair, staged, landed, qrow, qvec, masks, slots,
     load_sems, local_sems, send_sems, recv_sems) = rest
    at, core = position()
    partner = device(at, 1 - core)
    row, col = lax.axis_index("row"), lax.axis_index("col")
    zl, y = at["z"] % 2, at["y"]
    spread = [(a, b) for b in (2, 1, 3, 0) for a in (1, 0)]

    def there(a, b):
        return lax.rem(zl + a, 2), lax.rem(y + b, SIDE)

    def peer(a, b):
        far_z, far_y = there(a, b)
        return (row, far_z * 8 + far_y * 2 + core)

    meet = greet(
        [device(moved(at, dim, by), core) for dim in "xyz" for by in (1, -1, 2)]
        + [partner] + [peer(1, b) for b in (1, 2, 3)]
    )
    k0 = row * n_row_k
    total = q_hbm.shape[1]
    rows = mask_hbm.at[pl.ds(k0, n_row_k)]
    loads = [
        pltpu.make_async_copy(coeffs_hbm, coeffs, load_sems.at[0]),
        pltpu.make_async_copy(trial_hbm, trial, load_sems.at[1]),
        pltpu.make_async_copy(q_hbm.at[pl.ds(0, 1)], qrow, load_sems.at[2]),
        pltpu.make_async_copy(rows, masks.at[:, pl.ds(0, total)], load_sems.at[3]),
        pltpu.make_async_copy(rows, masks.at[:, pl.ds(total, total)], load_sems.at[4]),
        pltpu.make_async_copy(w_hbm, weights, load_sems.at[5]),
        pltpu.make_async_copy(q_hbm.at[pl.ds(0, 1)], qvec, load_sems.at[6]),
    ]
    for load in loads:
        load.start()
    for load in loads[:2]:
        load.wait()
    own[...] = lax.dot_general(
        trial[0], coeffs[0], (((1,), (1,)), ((), ())), preferred_element_type=jnp.float32
    ).astype(own.dtype)
    started, local = [], []

    def push(src, dst, to):
        k = len(started)
        copy = pltpu.make_async_remote_copy(
            src, dst, send_sems.at[k], recv_sems.at[k], device_id=to, device_id_type=MESH
        )
        copy.start()
        started.append(copy)
        return copy

    def keep(src, dst):
        copy = pltpu.make_async_copy(src, dst, local_sems.at[len(local)])
        copy.start()
        local.append(copy)
        return copy

    def coords(n, steps):
        return {d: None if by is None else moved(at, d, by)[d] for d, by in zip(PARTS[n][3], steps)}

    def region(n, steps):
        where = coords(n, steps)
        return bufs[n].at[tuple(pl.ds(0, SIDE) if where[d] is None else where[d] for d in PARTS[n][4])]

    def place(n, steps):
        where = coords(n, steps)
        h, rows, cols, _, _ = PARTS[n]
        spans = tuple(pl.ds(0, SIDE) if where[d] is None else where[d] for d in "xzy")
        dst = vecs[h].at[spans + (core, pl.ds(rows[0] - 16 * h, rows[1]), pl.ds(*cols))]
        src = region(n, steps)
        return push(src, dst, partner), keep(src, dst)

    def send(n, stage, steps, by, src=None):
        dim = PARTS[n][3][stage]
        block = region(n, steps)
        return push(block if src is None else src, block, device(moved(at, dim, by), core))

    def prepare():
        for load in loads[2:5]:
            load.wait()
        base = col * n_slots
        skip = turn[0] * n_slots

        def scan(j, carry):
            count, picked = carry
            q = qrow[0, j]
            held = (q >= base) & (q < base + n_slots)
            picked = tuple(jnp.where(held & (count == n), j, p) for n, p in enumerate(picked))
            return count + jnp.where(held, 1, 0), picked

        first = (-skip, (jnp.int32(-1),) * n_slots)
        _, picked = lax.fori_loop(0, total, scan, first, unroll=4)
        for n, p in enumerate(picked):
            slots[n] = p
        acc[...] = jnp.zeros_like(acc)
        loads[6].wait()
        first_q = n_slots * lax.broadcasted_iota(jnp.int32, (n_row_k, total), 0)
        held = (qvec[...] >= first_q) & (qvec[...] < first_q + n_slots)
        counts = jnp.sum(jnp.where(held, 1.0, 0.0), axis=1, keepdims=True)
        most[0] = jnp.max(counts).astype(jnp.int32)

    parts = range(len(PARTS))
    mine = [[n for n in parts if PARTS[n][0] == h] for h in range(HALVES)]
    own_piece = [own.at[pl.ds(*PARTS[n][1]), pl.ds(*PARTS[n][2])] for n in parts]
    kept = [keep(own_piece[n], region(n, (0, 0, 0))) for n in parts]
    meet()
    moving = [[send(n, 0, (0, 0, 0), by, own_piece[n]) for by in (2, 1, -1)] for n in parts]
    for copy in kept:
        copy.wait()
    for n in parts:
        for copy in moving[n]:
            copy.wait_recv()
        moving[n] = [send(n, 1, (None, 0, 0), by) for by in (2, 1, -1)]
    last = []
    for h in range(HALVES):
        for n in mine[h]:
            for copy in moving[n]:
                copy.wait_recv()
            last.append([send(n, 2, (None, None, 0), by) for by in (1, -1)])
        for n in mine[h]:
            last[n].append(send(n, 2, (None, None, 0), 2))
    placing = [[place(n, (None, None, 0)) for n in mine[h]] for h in range(HALVES)]
    prepare()

    def arrive(h):
        for k, by in enumerate((-1, 1, 2)):
            for n in mine[h]:
                last[n][k].wait_recv()
                placing[h].append(place(n, (None, None, by)))

    def settle(h):
        for there_copy, here_copy in placing[h]:
            there_copy.wait_recv()
            here_copy.wait()

    nv, rank = own.shape
    part_v = nv // HALVES

    def wrapped(k):
        return jnp.where(k >= total, k - total, k)

    def step(h):
        flat = vecs[h].reshape(total, part_v, rank)

        def side(start, scales):
            blocks = []
            for i in range(n_row_k):
                scale = jnp.full((part_v, rank), scales[i], jnp.float32).astype(own.dtype)
                blocks.append(flat[wrapped(start + i)] * scale)
            return jnp.concatenate(blocks, axis=0)

        def body(n, carry):
            slot = slots[n]
            used = jnp.where(slot >= 0, 1, 0)
            j = jnp.where(slot >= 0, slot, 0)
            w = weights[jnp.where(slot >= 0, qrow[0, j] - col * n_slots, 0)]
            ahead_k = wrapped(k0 + j)
            behind_k = wrapped(k0 + total - j)
            turned_used = jnp.where(slot > 0, 1, 0)
            ahead = [(used * masks[i, ahead_k + i]).astype(jnp.float32) for i in range(n_row_k)]
            behind = [
                (turned_used * (1 - masks[i, behind_k + i])).astype(jnp.float32) for i in range(n_row_k)
            ]
            direct = side(ahead_k, ahead)
            turned = side(behind_k, behind)
            both = lax.dot_general(
                direct, w, (((1,), (1,)), ((), ())), preferred_element_type=jnp.float32
            ) + jnp.dot(turned, w, preferred_element_type=jnp.float32)
            acc[h] += both.reshape(acc.shape[1:])
            return carry

        return body

    def mate(k, c):
        far_z, far_y = there(*spread[k])
        return far_z * 8 + far_y * 2 + c

    def swap(h):
        return [push(acc.at[h, mate(k, 1 - core)], pair.at[h, k], partner) for k in range(8)]

    sends = []

    def collect(h, swaps):
        for k in range(8):
            swaps[k].wait_recv()
            summed = acc[h, mate(k, core)] + pair[h, k]
            if k < 7:
                staged[h, k] = summed.astype(staged.dtype)
            if k > 0:
                sends.append(push(staged.at[h, k - 1], landed.at[h, k - 1], peer(*spread[k - 1])))
        return summed

    def finish(h, summed):
        for k in range(7):
            sends[h * 7 + k].wait_recv()
            summed += landed[h, k].astype(jnp.float32)
        high = summed.astype(jnp.bfloat16)
        low = (summed - high.astype(jnp.float32)).astype(jnp.bfloat16)
        out[0, pl.ds(h * part_v, part_v), :] = jnp.dot(
            high, coeffs[0], preferred_element_type=jnp.float32
        ) + jnp.dot(low, coeffs[0], preferred_element_type=jnp.float32)

    first, second = n_slots * 3 // 8, n_slots * 5 // 8
    arrive(0)
    loads[5].wait()
    settle(0)
    lax.fori_loop(0, first, step(0), 0)
    arrive(1)
    lax.fori_loop(first, n_slots, step(0), 0)
    early = swap(0)
    settle(1)
    lax.fori_loop(0, second, step(1), 0)
    summed0 = collect(0, early)
    lax.fori_loop(second, n_slots, step(1), 0)
    summed1 = collect(1, swap(1))
    finish(0, summed0)
    finish(1, summed1)
    for copy in started:
        copy.wait_send()


def run_round(turn, coeffs, trial, screened, qmap, mask):
    nv, rank, nt = trial.shape[1], coeffs.shape[1], coeffs.shape[2]
    n_slots = screened.shape[0]
    n_row_k = lax.axis_size("col")
    total = qmap.shape[0]
    part_v = nv // HALVES
    local = 5 * len(PARTS)
    remote = 13 * len(PARTS) + 15 * HALVES
    anywhere = pl.BlockSpec(memory_space=pl.ANY)
    return pl.pallas_call(
        lambda *refs: one_round(n_slots, n_row_k, *refs),
        out_shape=(
            jax.ShapeDtypeStruct((1, nv, nt), jnp.float32),
            jax.ShapeDtypeStruct((1,), jnp.int32),
        ),
        in_specs=[pl.BlockSpec(memory_space=pltpu.SMEM)] + [anywhere] * 5,
        out_specs=(pl.BlockSpec(memory_space=pltpu.VMEM), pl.BlockSpec(memory_space=pltpu.SMEM)),
        scratch_shapes=[
            pltpu.VMEM(coeffs.shape, coeffs.dtype),
            pltpu.VMEM(trial.shape, trial.dtype),
            pltpu.VMEM((nv, rank), jnp.bfloat16),
        ]
        + [pltpu.VMEM((SIDE, SIDE, SIDE, part[1][1], part[2][1]), jnp.bfloat16) for part in PARTS]
        + [
            pltpu.VMEM((SIDE, SIDE, SIDE, 2, part_v, rank), jnp.bfloat16) for _ in range(HALVES)
        ]
        + [
            pltpu.VMEM(screened.shape, screened.dtype),
            pltpu.VMEM((HALVES, n_row_k, part_v, rank), jnp.float32),
            pltpu.VMEM((HALVES, 8, part_v, rank), jnp.float32),
            pltpu.VMEM((HALVES, 7, part_v, rank), jnp.bfloat16),
            pltpu.VMEM((HALVES, 7, part_v, rank), jnp.bfloat16),
            pltpu.SMEM((1, total), jnp.int32),
            pltpu.VMEM((1, total), jnp.int32),
            pltpu.SMEM((n_row_k, 2 * total), jnp.int32),
            pltpu.SMEM((n_slots,), jnp.int32),
            pltpu.SemaphoreType.DMA((7,)),
            pltpu.SemaphoreType.DMA((local,)),
            pltpu.SemaphoreType.DMA((remote,)),
            pltpu.SemaphoreType.DMA((remote,)),
        ],
        compiler_params=pltpu.CompilerParams(
            collective_id=0, has_side_effects=True, vmem_limit_bytes=60 * 2**20
        ),
    )(turn, coeffs, trial, screened, qmap, mask)


def per_device(coeffs, trial, screened, qmap, mask):
    n_slots = screened.shape[0]
    args = (coeffs, trial, screened, qmap, mask)
    first, most = run_round(jnp.zeros((1,), jnp.int32), *args)

    def more(state):
        return state[0] * n_slots < most[0]

    def again(state):
        return state[0] + 1, state[1] + run_round(state[0][None], *args)[0]

    return lax.while_loop(more, again, (jnp.int32(1), first))[1]


def solution(mesh):
    return jax.shard_map(
        per_device,
        mesh=mesh,
        in_specs=(
            P(("row", "col"), None, None),
            P(("row", "col"), None, None),
            P("col", None, None),
            P(),
            P(),
        ),
        out_specs=P(("row", "col"), None, None),
        check_vma=False,
    )
```

```python
import jax
import jax.numpy as jnp
from jax import lax
from jax.experimental import pallas as pl
from jax.experimental.pallas import tpu as pltpu
from jax.sharding import PartitionSpec as P


MESH = pl.DeviceIdType.MESH
SIDE = 4
HALVES = 2
ORDERS = (("yzx", "xzy"), ("zxy", "yxz"), ("xyz", "zxy"))
PARTS = tuple(
    (h, (16 * h + r, n), cols, *ORDERS[(p + 2 * h) % 3])
    for h in range(HALVES)
    for p, (r, n, cols) in enumerate(((0, 8, (0, 384)), (8, 8, (0, 384)), (0, 16, (384, 128))))
)


def position():
    row, col = lax.axis_index("row"), lax.axis_index("col")
    return {"x": row // 2, "z": row % 2 * 2 + col // 8, "y": col % 8 // 2}, col % 2


def device(at, core):
    return (at["x"] * 2 + at["z"] // 2, at["z"] % 2 * 8 + at["y"] * 2 + core)


def moved(at, dim, by):
    return {**at, dim: lax.rem(at[dim] + SIDE + by, SIDE)}


def greet(peers):
    barrier = pltpu.get_barrier_semaphore()
    for peer in peers:
        pl.semaphore_signal(barrier, inc=1, device_id=peer, device_id_type=MESH)
    return lambda: pl.semaphore_wait(barrier, len(peers))


def one_round(n_slots, n_row_k, turn, coeffs_hbm, trial_hbm, w_hbm, q_hbm, mask_hbm, out, most,
              coeffs, trial, own, *rest):
    bufs, rest = rest[: len(PARTS)], rest[len(PARTS) :]
    vecs, rest = rest[:HALVES], rest[HALVES:]
    (weights, acc, pair, staged, landed, qrow, qvec, masks, slots,
     load_sems, local_sems, send_sems, recv_sems) = rest
    at, core = position()
    partner = device(at, 1 - core)
    row, col = lax.axis_index("row"), lax.axis_index("col")
    zl, y = at["z"] % 2, at["y"]
    spread = [(a, b) for b in (2, 1, 3, 0) for a in (1, 0)]

    def there(a, b):
        return lax.rem(zl + a, 2), lax.rem(y + b, SIDE)

    def peer(a, b):
        far_z, far_y = there(a, b)
        return (row, far_z * 8 + far_y * 2 + core)

    k0 = row * n_row_k
    total = q_hbm.shape[1]
    rows = mask_hbm.at[pl.ds(k0, n_row_k)]
    loads = [
        pltpu.make_async_copy(coeffs_hbm, coeffs, load_sems.at[0]),
        pltpu.make_async_copy(trial_hbm, trial, load_sems.at[1]),
        pltpu.make_async_copy(q_hbm.at[pl.ds(0, 1)], qrow, load_sems.at[2]),
        pltpu.make_async_copy(rows, masks.at[:, pl.ds(0, total)], load_sems.at[3]),
        pltpu.make_async_copy(rows, masks.at[:, pl.ds(total, total)], load_sems.at[4]),
        pltpu.make_async_copy(w_hbm, weights, load_sems.at[5]),
        pltpu.make_async_copy(q_hbm.at[pl.ds(0, 1)], qvec, load_sems.at[6]),
    ]
    for load in loads:
        load.start()
    meet = greet(
        [device(moved(at, dim, by), core) for dim in "xyz" for by in (1, -1, 2)]
        + [partner] + [peer(1, b) for b in (1, 2, 3)]
    )
    for load in loads[:2]:
        load.wait()
    own[...] = lax.dot_general(
        trial[0], coeffs[0], (((1,), (1,)), ((), ())), preferred_element_type=jnp.float32
    ).astype(own.dtype)
    started, local = [], []

    def push(src, dst, to):
        k = len(started)
        copy = pltpu.make_async_remote_copy(
            src, dst, send_sems.at[k], recv_sems.at[k], device_id=to, device_id_type=MESH
        )
        copy.start()
        started.append(copy)
        return copy

    def keep(src, dst):
        copy = pltpu.make_async_copy(src, dst, local_sems.at[len(local)])
        copy.start()
        local.append(copy)
        return copy

    def coords(n, steps):
        return {d: None if by is None else moved(at, d, by)[d] for d, by in zip(PARTS[n][3], steps)}

    def region(n, steps):
        where = coords(n, steps)
        return bufs[n].at[tuple(pl.ds(0, SIDE) if where[d] is None else where[d] for d in PARTS[n][4])]

    def place(n, steps):
        where = coords(n, steps)
        h, rows, cols, _, _ = PARTS[n]
        spans = tuple(pl.ds(0, SIDE) if where[d] is None else where[d] for d in "xzy")
        dst = vecs[h].at[spans + (core, pl.ds(rows[0] - 16 * h, rows[1]), pl.ds(*cols))]
        src = region(n, steps)
        return push(src, dst, partner), keep(src, dst)

    def send(n, stage, steps, by, src=None):
        dim = PARTS[n][3][stage]
        block = region(n, steps)
        return push(block if src is None else src, block, device(moved(at, dim, by), core))

    def prepare():
        for load in loads[2:5]:
            load.wait()
        base = col * n_slots
        skip = turn[0] * n_slots

        def scan(j, carry):
            count, picked = carry
            q = qrow[0, j]
            held = (q >= base) & (q < base + n_slots)
            picked = tuple(jnp.where(held & (count == n), j, p) for n, p in enumerate(picked))
            return count + jnp.where(held, 1, 0), picked

        first = (-skip, (jnp.int32(-1),) * n_slots)
        _, picked = lax.fori_loop(0, total, scan, first, unroll=4)
        for n, p in enumerate(picked):
            slots[n] = p
        acc[...] = jnp.zeros_like(acc)
        loads[6].wait()
        first_q = n_slots * lax.broadcasted_iota(jnp.int32, (n_row_k, total), 0)
        held = (qvec[...] >= first_q) & (qvec[...] < first_q + n_slots)
        counts = jnp.sum(jnp.where(held, 1.0, 0.0), axis=1, keepdims=True)
        most[0] = jnp.max(counts).astype(jnp.int32)

    parts = range(len(PARTS))
    mine = [[n for n in parts if PARTS[n][0] == h] for h in range(HALVES)]
    own_piece = [own.at[pl.ds(*PARTS[n][1]), pl.ds(*PARTS[n][2])] for n in parts]
    kept = [keep(own_piece[n], region(n, (0, 0, 0))) for n in parts]
    meet()
    moving = [[send(n, 0, (0, 0, 0), by, own_piece[n]) for by in (2, 1, -1)] for n in parts]
    for copy in kept:
        copy.wait()
    for n in parts:
        for copy in moving[n]:
            copy.wait_recv()
        moving[n] = [send(n, 1, (None, 0, 0), by) for by in (2, 1, -1)]
    last = []
    for h in range(HALVES):
        for n in mine[h]:
            for copy in moving[n]:
                copy.wait_recv()
            last.append([send(n, 2, (None, None, 0), by) for by in (1, -1)])
        for n in mine[h]:
            last[n].append(send(n, 2, (None, None, 0), 2))
    placing = [[place(n, (None, None, 0)) for n in mine[h]] for h in range(HALVES)]
    prepare()

    def arrive(h):
        for k, by in enumerate((-1, 1, 2)):
            for n in mine[h]:
                last[n][k].wait_recv()
                placing[h].append(place(n, (None, None, by)))

    def settle(h):
        for there_copy, here_copy in placing[h]:
            there_copy.wait_recv()
            here_copy.wait()

    nv, rank = own.shape
    part_v = nv // HALVES

    def wrapped(k):
        return jnp.where(k >= total, k - total, k)

    def step(h):
        flat = vecs[h].reshape(total, part_v, rank)

        def side(start, scales):
            blocks = []
            for i in range(n_row_k):
                scale = jnp.full((part_v, rank), scales[i], jnp.float32).astype(own.dtype)
                blocks.append(flat[wrapped(start + i)] * scale)
            return jnp.concatenate(blocks, axis=0)

        def body(n, carry):
            slot = slots[n]
            used = jnp.where(slot >= 0, 1, 0)
            j = jnp.where(slot >= 0, slot, 0)
            w = weights[jnp.where(slot >= 0, qrow[0, j] - col * n_slots, 0)]
            ahead_k = wrapped(k0 + j)
            behind_k = wrapped(k0 + total - j)
            turned_used = jnp.where(slot > 0, 1, 0)
            ahead = [(used * masks[i, ahead_k + i]).astype(jnp.float32) for i in range(n_row_k)]
            behind = [
                (turned_used * (1 - masks[i, behind_k + i])).astype(jnp.float32) for i in range(n_row_k)
            ]
            direct = side(ahead_k, ahead)
            turned = side(behind_k, behind)
            both = lax.dot_general(
                direct, w, (((1,), (1,)), ((), ())), preferred_element_type=jnp.float32
            ) + jnp.dot(turned, w, preferred_element_type=jnp.float32)
            acc[h] += both.reshape(acc.shape[1:])
            return carry

        return body

    def mate(k, c):
        far_z, far_y = there(*spread[k])
        return far_z * 8 + far_y * 2 + c

    def swap(h):
        return [push(acc.at[h, mate(k, 1 - core)], pair.at[h, k], partner) for k in range(8)]

    sends = []

    def collect(h, swaps):
        for k in range(8):
            swaps[k].wait_recv()
            summed = acc[h, mate(k, core)] + pair[h, k]
            if k < 7:
                staged[h, k] = summed.astype(staged.dtype)
            if k > 0:
                sends.append(push(staged.at[h, k - 1], landed.at[h, k - 1], peer(*spread[k - 1])))
        return summed

    def finish(h, summed):
        for k in range(7):
            sends[h * 7 + k].wait_recv()
            summed += landed[h, k].astype(jnp.float32)
        high = summed.astype(jnp.bfloat16)
        low = (summed - high.astype(jnp.float32)).astype(jnp.bfloat16)
        out[0, pl.ds(h * part_v, part_v), :] = jnp.dot(
            high, coeffs[0], preferred_element_type=jnp.float32
        ) + jnp.dot(low, coeffs[0], preferred_element_type=jnp.float32)

    first, second = n_slots * 3 // 8, n_slots * 5 // 8
    arrive(0)
    loads[5].wait()
    settle(0)
    lax.fori_loop(0, first, step(0), 0)
    arrive(1)
    lax.fori_loop(first, n_slots, step(0), 0)
    early = swap(0)
    settle(1)
    lax.fori_loop(0, second, step(1), 0)
    summed0 = collect(0, early)
    lax.fori_loop(second, n_slots, step(1), 0)
    summed1 = collect(1, swap(1))
    finish(0, summed0)
    finish(1, summed1)
    for copy in started:
        copy.wait_send()


def run_round(turn, coeffs, trial, screened, qmap, mask):
    nv, rank, nt = trial.shape[1], coeffs.shape[1], coeffs.shape[2]
    n_slots = screened.shape[0]
    n_row_k = lax.axis_size("col")
    total = qmap.shape[0]
    part_v = nv // HALVES
    local = 5 * len(PARTS)
    remote = 13 * len(PARTS) + 15 * HALVES
    anywhere = pl.BlockSpec(memory_space=pl.ANY)
    return pl.pallas_call(
        lambda *refs: one_round(n_slots, n_row_k, *refs),
        out_shape=(
            jax.ShapeDtypeStruct((1, nv, nt), jnp.float32),
            jax.ShapeDtypeStruct((1,), jnp.int32),
        ),
        in_specs=[pl.BlockSpec(memory_space=pltpu.SMEM)] + [anywhere] * 5,
        out_specs=(pl.BlockSpec(memory_space=pltpu.VMEM), pl.BlockSpec(memory_space=pltpu.SMEM)),
        scratch_shapes=[
            pltpu.VMEM(coeffs.shape, coeffs.dtype),
            pltpu.VMEM(trial.shape, trial.dtype),
            pltpu.VMEM((nv, rank), jnp.bfloat16),
        ]
        + [pltpu.VMEM((SIDE, SIDE, SIDE, part[1][1], part[2][1]), jnp.bfloat16) for part in PARTS]
        + [
            pltpu.VMEM((SIDE, SIDE, SIDE, 2, part_v, rank), jnp.bfloat16) for _ in range(HALVES)
        ]
        + [
            pltpu.VMEM(screened.shape, screened.dtype),
            pltpu.VMEM((HALVES, n_row_k, part_v, rank), jnp.float32),
            pltpu.VMEM((HALVES, 8, part_v, rank), jnp.float32),
            pltpu.VMEM((HALVES, 7, part_v, rank), jnp.bfloat16),
            pltpu.VMEM((HALVES, 7, part_v, rank), jnp.bfloat16),
            pltpu.SMEM((1, total), jnp.int32),
            pltpu.VMEM((1, total), jnp.int32),
            pltpu.SMEM((n_row_k, 2 * total), jnp.int32),
            pltpu.SMEM((n_slots,), jnp.int32),
            pltpu.SemaphoreType.DMA((7,)),
            pltpu.SemaphoreType.DMA((local,)),
            pltpu.SemaphoreType.DMA((remote,)),
            pltpu.SemaphoreType.DMA((remote,)),
        ],
        compiler_params=pltpu.CompilerParams(
            collective_id=0, has_side_effects=True, vmem_limit_bytes=60 * 2**20
        ),
    )(turn, coeffs, trial, screened, qmap, mask)


def per_device(coeffs, trial, screened, qmap, mask):
    n_slots = screened.shape[0]
    args = (coeffs, trial, screened, qmap, mask)
    first, most = run_round(jnp.zeros((1,), jnp.int32), *args)

    def more(state):
        return state[0] * n_slots < most[0]

    def again(state):
        return state[0] + 1, state[1] + run_round(state[0][None], *args)[0]

    return lax.while_loop(more, again, (jnp.int32(1), first))[1]


def solution(mesh):
    return jax.shard_map(
        per_device,
        mesh=mesh,
        in_specs=(
            P(("row", "col"), None, None),
            P(("row", "col"), None, None),
            P("col", None, None),
            P(),
            P(),
        ),
        out_specs=P(("row", "col"), None, None),
        check_vma=False,
    )
```

```python
import jax
import jax.numpy as jnp
from jax import lax
from jax.experimental import pallas as pl
from jax.experimental.pallas import tpu as pltpu
from jax.sharding import PartitionSpec as P


MESH = pl.DeviceIdType.MESH
SIDE = 4
HALVES = 2
ORDERS = (("yzx", "xzy"), ("zxy", "yxz"), ("xyz", "zxy"))
PARTS = tuple(
    (h, (16 * h + r, n), cols, *ORDERS[(p + 2 * h) % 3])
    for h in range(HALVES)
    for p, (r, n, cols) in enumerate(((0, 8, (0, 384)), (8, 8, (0, 384)), (0, 16, (384, 128))))
)


def position():
    row, col = lax.axis_index("row"), lax.axis_index("col")
    return {"x": row // 2, "z": row % 2 * 2 + col // 8, "y": col % 8 // 2}, col % 2


def device(at, core):
    return (at["x"] * 2 + at["z"] // 2, at["z"] % 2 * 8 + at["y"] * 2 + core)


def moved(at, dim, by):
    return {**at, dim: lax.rem(at[dim] + SIDE + by, SIDE)}


def greet(peers):
    barrier = pltpu.get_barrier_semaphore()
    for peer in peers:
        pl.semaphore_signal(barrier, inc=1, device_id=peer, device_id_type=MESH)
    return lambda: pl.semaphore_wait(barrier, len(peers))


def one_round(n_slots, n_row_k, turn, coeffs_hbm, trial_hbm, w_hbm, q_hbm, mask_hbm, out, most,
              coeffs, trial, own, *rest):
    bufs, rest = rest[: len(PARTS)], rest[len(PARTS) :]
    vecs, rest = rest[:HALVES], rest[HALVES:]
    (weights, acc, pair, staged, landed, qrow, qvec, masks, slots,
     load_sems, local_sems, send_sems, recv_sems) = rest
    at, core = position()
    partner = device(at, 1 - core)
    row, col = lax.axis_index("row"), lax.axis_index("col")
    zl, y = at["z"] % 2, at["y"]
    spread = [(a, b) for b in (2, 1, 3, 0) for a in (1, 0)]

    def there(a, b):
        return lax.rem(zl + a, 2), lax.rem(y + b, SIDE)

    def peer(a, b):
        far_z, far_y = there(a, b)
        return (row, far_z * 8 + far_y * 2 + core)

    k0 = row * n_row_k
    total = q_hbm.shape[1]
    rows = mask_hbm.at[pl.ds(k0, n_row_k)]
    loads = [
        pltpu.make_async_copy(coeffs_hbm, coeffs, load_sems.at[0]),
        pltpu.make_async_copy(trial_hbm, trial, load_sems.at[1]),
        pltpu.make_async_copy(q_hbm.at[pl.ds(0, 1)], qrow, load_sems.at[2]),
        pltpu.make_async_copy(rows, masks.at[:, pl.ds(0, total)], load_sems.at[3]),
        pltpu.make_async_copy(rows, masks.at[:, pl.ds(total, total)], load_sems.at[4]),
        pltpu.make_async_copy(w_hbm, weights, load_sems.at[5]),
        pltpu.make_async_copy(q_hbm.at[pl.ds(0, 1)], qvec, load_sems.at[6]),
    ]
    for load in loads:
        load.start()
    meet = greet(
        [device(moved(at, dim, by), core) for dim in "xyz" for by in (1, -1, 2)]
        + [partner] + [peer(1, b) for b in (1, 2, 3)]
    )
    for load in loads[:2]:
        load.wait()
    own[...] = lax.dot_general(
        trial[0], coeffs[0], (((1,), (1,)), ((), ())), preferred_element_type=jnp.float32
    ).astype(own.dtype)
    started, local = [], []

    def push(src, dst, to):
        k = len(started)
        copy = pltpu.make_async_remote_copy(
            src, dst, send_sems.at[k], recv_sems.at[k], device_id=to, device_id_type=MESH
        )
        copy.start()
        started.append(copy)
        return copy

    def keep(src, dst):
        copy = pltpu.make_async_copy(src, dst, local_sems.at[len(local)])
        copy.start()
        local.append(copy)
        return copy

    def coords(n, steps):
        return {d: None if by is None else moved(at, d, by)[d] for d, by in zip(PARTS[n][3], steps)}

    def region(n, steps):
        where = coords(n, steps)
        return bufs[n].at[tuple(pl.ds(0, SIDE) if where[d] is None else where[d] for d in PARTS[n][4])]

    def place(n, steps):
        where = coords(n, steps)
        h, rows, cols, _, _ = PARTS[n]
        spans = tuple(pl.ds(0, SIDE) if where[d] is None else where[d] for d in "xzy")
        dst = vecs[h].at[spans + (core, pl.ds(rows[0] - 16 * h, rows[1]), pl.ds(*cols))]
        src = region(n, steps)
        return push(src, dst, partner), keep(src, dst)

    def send(n, stage, steps, by, src=None):
        dim = PARTS[n][3][stage]
        block = region(n, steps)
        return push(block if src is None else src, block, device(moved(at, dim, by), core))

    def prepare():
        for load in loads[2:5]:
            load.wait()
        base = col * n_slots
        skip = turn[0] * n_slots

        def scan(j, carry):
            count, picked = carry
            q = qrow[0, j]
            held = (q >= base) & (q < base + n_slots)
            picked = tuple(jnp.where(held & (count == n), j, p) for n, p in enumerate(picked))
            return count + jnp.where(held, 1, 0), picked

        first = (-skip, (jnp.int32(-1),) * n_slots)
        _, picked = lax.fori_loop(0, total, scan, first, unroll=4)
        for n, p in enumerate(picked):
            slots[n] = p
        acc[...] = jnp.zeros_like(acc)
        loads[6].wait()
        first_q = n_slots * lax.broadcasted_iota(jnp.int32, (n_row_k, total), 0)
        held = (qvec[...] >= first_q) & (qvec[...] < first_q + n_slots)
        counts = jnp.sum(jnp.where(held, 1.0, 0.0), axis=1, keepdims=True)
        most[0] = jnp.max(counts).astype(jnp.int32)

    parts = range(len(PARTS))
    mine = [[n for n in parts if PARTS[n][0] == h] for h in range(HALVES)]
    own_piece = [own.at[pl.ds(*PARTS[n][1]), pl.ds(*PARTS[n][2])] for n in parts]
    kept = [keep(own_piece[n], region(n, (0, 0, 0))) for n in parts]
    meet()
    moving = [[send(n, 0, (0, 0, 0), by, own_piece[n]) for by in (2, 1, -1)] for n in parts]
    for copy in kept:
        copy.wait()
    for n in parts:
        for copy in moving[n]:
            copy.wait_recv()
        moving[n] = [send(n, 1, (None, 0, 0), by) for by in (2, 1, -1)]
    last = []
    for h in range(HALVES):
        for n in mine[h]:
            for copy in moving[n]:
                copy.wait_recv()
            last.append([send(n, 2, (None, None, 0), by) for by in (1, -1)])
        for n in mine[h]:
            last[n].append(send(n, 2, (None, None, 0), 2))
    placing = [[place(n, (None, None, 0)) for n in mine[h]] for h in range(HALVES)]
    prepare()

    def arrive(h):
        for k, by in enumerate((-1, 1, 2)):
            for n in mine[h]:
                last[n][k].wait_recv()
                placing[h].append(place(n, (None, None, by)))

    def settle(h):
        for there_copy, here_copy in placing[h]:
            there_copy.wait_recv()
            here_copy.wait()

    nv, rank = own.shape
    part_v = nv // HALVES

    def wrapped(k):
        return jnp.where(k >= total, k - total, k)

    def step(h):
        flat = vecs[h].reshape(total, part_v, rank)

        def side(start, scales):
            blocks = []
            for i in range(n_row_k):
                scale = jnp.full((part_v, rank), scales[i], jnp.float32).astype(own.dtype)
                blocks.append(flat[wrapped(start + i)] * scale)
            return jnp.concatenate(blocks, axis=0)

        def body(n, carry):
            slot = slots[n]
            used = jnp.where(slot >= 0, 1, 0)
            j = jnp.where(slot >= 0, slot, 0)
            w = weights[jnp.where(slot >= 0, qrow[0, j] - col * n_slots, 0)]
            ahead_k = wrapped(k0 + j)
            behind_k = wrapped(k0 + total - j)
            turned_used = jnp.where(slot > 0, 1, 0)
            ahead = [(used * masks[i, ahead_k + i]).astype(jnp.float32) for i in range(n_row_k)]
            behind = [
                (turned_used * (1 - masks[i, behind_k + i])).astype(jnp.float32) for i in range(n_row_k)
            ]
            direct = side(ahead_k, ahead)
            turned = side(behind_k, behind)
            both = lax.dot_general(
                direct, w, (((1,), (1,)), ((), ())), preferred_element_type=jnp.float32
            ) + jnp.dot(turned, w, preferred_element_type=jnp.float32)
            acc[h] += both.reshape(acc.shape[1:])
            return carry

        return body

    def mate(k, c):
        far_z, far_y = there(*spread[k])
        return far_z * 8 + far_y * 2 + c

    def swap(h):
        return [push(acc.at[h, mate(k, 1 - core)], pair.at[h, k], partner) for k in range(8)]

    sends = []

    def collect(h, swaps):
        for k in range(8):
            swaps[k].wait_recv()
            summed = acc[h, mate(k, core)] + pair[h, k]
            if k < 7:
                staged[h, k] = summed.astype(staged.dtype)
            if k > 0:
                sends.append(push(staged.at[h, k - 1], landed.at[h, k - 1], peer(*spread[k - 1])))
        return summed

    def finish(h, summed):
        for k in range(7):
            sends[h * 7 + k].wait_recv()
            summed += landed[h, k].astype(jnp.float32)
        high = summed.astype(jnp.bfloat16)
        low = (summed - high.astype(jnp.float32)).astype(jnp.bfloat16)
        out[0, pl.ds(h * part_v, part_v), :] = jnp.dot(
            high, coeffs[0], preferred_element_type=jnp.float32
        ) + jnp.dot(low, coeffs[0], preferred_element_type=jnp.float32)

    first, second = n_slots * 3 // 8, n_slots * 4 // 8
    arrive(0)
    loads[5].wait()
    settle(0)
    lax.fori_loop(0, first, step(0), 0)
    arrive(1)
    lax.fori_loop(first, n_slots, step(0), 0)
    early = swap(0)
    settle(1)
    lax.fori_loop(0, second, step(1), 0)
    summed0 = collect(0, early)
    lax.fori_loop(second, n_slots, step(1), 0)
    summed1 = collect(1, swap(1))
    finish(0, summed0)
    finish(1, summed1)
    for copy in started:
        copy.wait_send()


def run_round(turn, coeffs, trial, screened, qmap, mask):
    nv, rank, nt = trial.shape[1], coeffs.shape[1], coeffs.shape[2]
    n_slots = screened.shape[0]
    n_row_k = lax.axis_size("col")
    total = qmap.shape[0]
    part_v = nv // HALVES
    local = 5 * len(PARTS)
    remote = 13 * len(PARTS) + 15 * HALVES
    anywhere = pl.BlockSpec(memory_space=pl.ANY)
    return pl.pallas_call(
        lambda *refs: one_round(n_slots, n_row_k, *refs),
        out_shape=(
            jax.ShapeDtypeStruct((1, nv, nt), jnp.float32),
            jax.ShapeDtypeStruct((1,), jnp.int32),
        ),
        in_specs=[pl.BlockSpec(memory_space=pltpu.SMEM)] + [anywhere] * 5,
        out_specs=(pl.BlockSpec(memory_space=pltpu.VMEM), pl.BlockSpec(memory_space=pltpu.SMEM)),
        scratch_shapes=[
            pltpu.VMEM(coeffs.shape, coeffs.dtype),
            pltpu.VMEM(trial.shape, trial.dtype),
            pltpu.VMEM((nv, rank), jnp.bfloat16),
        ]
        + [pltpu.VMEM((SIDE, SIDE, SIDE, part[1][1], part[2][1]), jnp.bfloat16) for part in PARTS]
        + [
            pltpu.VMEM((SIDE, SIDE, SIDE, 2, part_v, rank), jnp.bfloat16) for _ in range(HALVES)
        ]
        + [
            pltpu.VMEM(screened.shape, screened.dtype),
            pltpu.VMEM((HALVES, n_row_k, part_v, rank), jnp.float32),
            pltpu.VMEM((HALVES, 8, part_v, rank), jnp.float32),
            pltpu.VMEM((HALVES, 7, part_v, rank), jnp.bfloat16),
            pltpu.VMEM((HALVES, 7, part_v, rank), jnp.bfloat16),
            pltpu.SMEM((1, total), jnp.int32),
            pltpu.VMEM((1, total), jnp.int32),
            pltpu.SMEM((n_row_k, 2 * total), jnp.int32),
            pltpu.SMEM((n_slots,), jnp.int32),
            pltpu.SemaphoreType.DMA((7,)),
            pltpu.SemaphoreType.DMA((local,)),
            pltpu.SemaphoreType.DMA((remote,)),
            pltpu.SemaphoreType.DMA((remote,)),
        ],
        compiler_params=pltpu.CompilerParams(
            collective_id=0, has_side_effects=True, vmem_limit_bytes=60 * 2**20
        ),
    )(turn, coeffs, trial, screened, qmap, mask)


def per_device(coeffs, trial, screened, qmap, mask):
    n_slots = screened.shape[0]
    args = (coeffs, trial, screened, qmap, mask)
    first, most = run_round(jnp.zeros((1,), jnp.int32), *args)

    def more(state):
        return state[0] * n_slots < most[0]

    def again(state):
        return state[0] + 1, state[1] + run_round(state[0][None], *args)[0]

    return lax.while_loop(more, again, (jnp.int32(1), first))[1]


def solution(mesh):
    return jax.shard_map(
        per_device,
        mesh=mesh,
        in_specs=(
            P(("row", "col"), None, None),
            P(("row", "col"), None, None),
            P("col", None, None),
            P(),
            P(),
        ),
        out_specs=P(("row", "col"), None, None),
        check_vma=False,
    )
```
